32 devices in a mesh: series: 16 (over z, y, core), mp: 2 (over x).
Axes of the slice: x: 2, y: 2, z: 4, core: 2. Of those that a mesh axis runs over, the one named last changes fastest.
Arguments:
- series_in: bfloat16 [256, 256, 768], P('series'), may hold values from -6 to 6
- norm_gain: float32 [768], replicated, may hold values from 0.5 to 1.5
- w_time: bfloat16 [768, 12, 192], P(None, 'mp'), may hold values from -0.375 to 0.375
- w_group: bfloat16 [768, 12, 192], P(None, 'mp'), may hold values from -0.375 to 0.375
- w_gate: bfloat16 [768, 768], P(None, 'mp'), may hold values from -0.4375 to 0.4375
- w_out: bfloat16 [768, 768], P('mp'), may hold values from -0.4375 to 0.4375
- group_of: int32 [256], replicated, may hold values from 0 to 7, as said below
Outputs:
- block_out: bfloat16 [256, 256, 768], P('series', None, 'mp')
The draws below stay inside these ranges and needn't reach their ends.
Inputs may be any that keep to these rules, and one draw needn't show every extreme that they name: `group_of`: groups are numbered from 0 without gaps; each holds 8 to 64 series, one group exactly 8 and one exactly 64; members are spread over the series at random.
All inputs are finite; a program needn't handle non-finite values.
Results may differ from the reference program's by a relative error of at most 0.015.
Values may be sent and summed in bfloat16 or wider, within the bound.
A program may use at most 128 MiB of HBM per device.

```python
import jax
import jax.numpy as jnp
from jax import lax

D = 768
HEADS = 12
HD = 64
SER_DEV = 16
P_SIZE = 256
GROUP_MIN = 8
GROUP_MAX = 64
SERIES = 256
HEADS_DEV = 6
N_SERIES = 16
N_MP = 2


def draw_group_of(key, part):
    key_sizes = jax.random.fold_in(key, 11)
    key_order = jax.random.fold_in(key, 23)
    mean_size = (GROUP_MIN + GROUP_MAX) // 2
    rest_series = SERIES - GROUP_MIN - GROUP_MAX
    other_count = (rest_series + mean_size - 1) // mean_size
    slot_index = jnp.arange(other_count)
    base_sizes = rest_series // other_count + (slot_index < rest_series % other_count).astype(jnp.int32)
    pair_count = other_count // 2
    if pair_count > 0:
        donors = base_sizes[0:2 * pair_count:2]
        takers = base_sizes[1:2 * pair_count:2]
        limits = jnp.minimum(donors - GROUP_MIN, GROUP_MAX - takers)
        moved = jax.random.randint(key_sizes, (pair_count,), 0, limits + 1)
        base_sizes = base_sizes.at[0:2 * pair_count:2].add(-moved)
        base_sizes = base_sizes.at[1:2 * pair_count:2].add(moved)
    group_sizes = jnp.concatenate([jnp.array([GROUP_MIN, GROUP_MAX], jnp.int32), base_sizes.astype(jnp.int32)])
    group_ends = jnp.cumsum(group_sizes)
    position = jnp.arange(SERIES)
    group_index = jnp.sum((position[:, None] >= group_ends[None, :]).astype(jnp.int32), axis=1)
    shuffle = jax.random.permutation(key_order, SERIES)
    return group_index[jnp.argsort(shuffle)].astype(jnp.int32)


def shard_levels(stream_key, shape, cuts, least, top_value):
    def one(axis_at, shards_of):
        draws = jax.random.uniform(jax.random.fold_in(jax.random.fold_in(stream_key, 6), axis_at), (shards_of,), jnp.float32, least / len(cuts), top_value / len(cuts))
        return jnp.repeat(jnp.exp(draws), shape[axis_at] // shards_of).reshape((-1,) + (1,) * (len(shape) - axis_at - 1))

    factor_of = one(*cuts[0])
    for cut in cuts[1:]:
        factor_of = factor_of * one(*cut)
    return factor_of


def noise(key, extent, deviation, limit, pieces=(), dtype=jnp.bfloat16):
    entries = jax.random.normal(key, extent, jnp.float32) * deviation
    if len(pieces) > 0:
        entries = shard_levels(key, extent, pieces, -0.22, 0.18) * entries
    return jnp.clip(entries, min=-limit, max=limit).astype(dtype)


def setup_inputs(seed: int = 0) -> dict:
    splits = jax.random.split(jax.random.key(seed), 8)
    series_in = noise(splits[0], (SERIES, P_SIZE, D), 1.0, 6.0, ((0, 16),))
    norm_gain = jnp.clip(1.0 + 0.1 * jax.random.normal(splits[1], (D,), jnp.float32), 0.5, 1.5)
    w_time = noise(splits[2], (D, HEADS, 3 * HD), (D // 3) ** -0.5, 0.375, ((1, 2),))
    w_group = noise(splits[3], (D, HEADS, 3 * HD), (D // 3) ** -0.5, 0.375, ((1, 2),))
    w_gate = noise(splits[4], (D, HEADS * HD), (D // 4) ** -0.5, 0.4375, ((1, 2),))
    w_out = noise(splits[5], (HEADS * HD, D), (HEADS * HD // 4) ** -0.5, 0.4375, ((0, 2),))
    group_of = draw_group_of(jax.random.fold_in(splits[7], 71), 0)
    return {"series_in": series_in, "norm_gain": norm_gain, "w_time": w_time, "w_group": w_group, "w_gate": w_gate, "w_out": w_out, "group_of": group_of}


def rms_norm(series_in, norm_gain):
    values_f = series_in.astype(jnp.float32)
    mean_sq = lax.optimization_barrier(jnp.mean(values_f * values_f, axis=-1, keepdims=True))
    return (values_f * lax.rsqrt(mean_sq + 1e-06) * norm_gain.astype(jnp.float32)).astype(jnp.bfloat16)

def time_block(block_qkv):
    queries = block_qkv[:, :, :, 0].astype(jnp.float32)
    keys_in = block_qkv[:, :, :, 1].astype(jnp.float32)
    values_in = block_qkv[:, :, :, 2].astype(jnp.float32)
    scores = jnp.einsum('bphd,bqhd->bhpq', queries, keys_in) * HD ** (-0.5)
    weights = lax.optimization_barrier(jax.nn.softmax(scores, axis=-1).astype(jnp.bfloat16))
    return jnp.einsum('bhpq,bqhd->bphd', weights.astype(jnp.float32), values_in).astype(jnp.bfloat16)

def group_patch(patch_qkv, same_group):
    queries = patch_qkv[:, :, 0].astype(jnp.float32)
    keys_in = patch_qkv[:, :, 1].astype(jnp.float32)
    values_in = patch_qkv[:, :, 2].astype(jnp.float32)
    scores = jnp.einsum('ihd,jhd->hij', queries, keys_in) * HD ** (-0.5)
    scores = jnp.where(same_group[None], scores, -1e+30)
    weights = lax.optimization_barrier(jax.nn.softmax(scores, axis=-1).astype(jnp.bfloat16))
    return jnp.einsum('hij,jhd->ihd', weights.astype(jnp.float32), values_in).astype(jnp.bfloat16)

def reference(series_in, norm_gain, w_time, w_group, w_gate, w_out, group_of):
    normed = rms_norm(series_in, norm_gain)
    flat_rows = normed.reshape(SERIES * P_SIZE, D)
    time_qkv = jnp.dot(flat_rows, w_time.reshape(D, -1), preferred_element_type=jnp.float32).astype(jnp.bfloat16)
    time_qkv = time_qkv.reshape(N_SERIES, SER_DEV, P_SIZE, HEADS, 3, HD)
    time_out = lax.map(time_block, time_qkv).reshape(SERIES * P_SIZE, HEADS * HD)
    group_qkv = jnp.dot(flat_rows, w_group.reshape(D, -1), preferred_element_type=jnp.float32).astype(jnp.bfloat16)
    group_qkv = group_qkv.reshape(SERIES, P_SIZE, HEADS, 3, HD)
    same_group = group_of[:, None] == group_of[None, :]
    group_out = lax.map(lambda patch_qkv: group_patch(patch_qkv, same_group), jnp.moveaxis(group_qkv, 1, 0))
    group_out = jnp.moveaxis(group_out, 0, 1).reshape(SERIES * P_SIZE, HEADS * HD)
    gate_value = jax.nn.sigmoid(jnp.dot(flat_rows, w_gate, preferred_element_type=jnp.float32))
    merged = (time_out.astype(jnp.float32) + gate_value * group_out.astype(jnp.float32)).astype(jnp.bfloat16)
    width_dev = HEADS_DEV * HD
    total_sum = jnp.zeros((SERIES * P_SIZE, D), jnp.float32)
    for member in range(N_MP):
        head_term = jnp.dot(merged[:, member * width_dev:(member + 1) * width_dev], w_out[member * width_dev:(member + 1) * width_dev], preferred_element_type=jnp.float32)
        total_sum = total_sum + head_term.astype(jnp.bfloat16).astype(jnp.float32)
    return total_sum.astype(jnp.bfloat16).reshape(SERIES, P_SIZE, D)
```

```python
from functools import partial

import jax
import jax.numpy as jnp
from jax import lax
from jax.experimental import pallas as pl
from jax.experimental.pallas import tpu as pltpu
from jax.sharding import PartitionSpec as P

CHUNKS = 1
VMEM_BYTES = 60 * 1024 * 1024


def rms_norm(series_in, norm_gain):
    values_f = series_in.astype(jnp.float32)
    mean_sq = jnp.mean(values_f * values_f, axis=-1, keepdims=True)
    return (values_f * lax.rsqrt(mean_sq + 1e-06) * norm_gain).astype(jnp.bfloat16)


def attend_pair(queries, keys_in, values_in, bias, head_size):
    rows = queries.shape[0]
    lane = lax.broadcasted_iota(jnp.int32, queries.shape, 1)
    first = lane < head_size
    zero = jnp.zeros_like(queries)
    ones = jnp.ones_like(values_in)
    extended = jnp.concatenate([values_in, ones], axis=1)
    outs = []
    for own in (jnp.where(first, queries, zero), jnp.where(first, zero, queries)):
        scores = lax.dot_general(
            own, keys_in, (((1,), (1,)), ((), ())), preferred_element_type=jnp.float32
        )
        if bias is not None:
            scores = scores + bias
        top = jnp.max(scores, axis=1, keepdims=True)
        weights = jnp.exp(scores - top).astype(jnp.bfloat16)
        outs.append(jnp.dot(weights, extended, preferred_element_type=jnp.float32))
    pair = values_in.shape[1]
    sums = jnp.where(first, outs[0][:, pair:], outs[1][:, pair:])
    tops = jnp.where(first, outs[0][:, :pair], outs[1][:, :pair])
    return tops / sums


def time_kernel(x_ref, gain_ref, w_ref, out_ref, *, head_size):
    normed = rms_norm(x_ref[0], gain_ref[...])
    width = out_ref.shape[-1]
    pair = 2 * head_size
    scale = head_size ** (-0.5)
    qkv = jnp.dot(normed, w_ref[...], preferred_element_type=jnp.float32)
    queries = (qkv[:, :width].astype(jnp.bfloat16) * scale).astype(jnp.bfloat16)
    keys_in = qkv[:, width : 2 * width].astype(jnp.bfloat16)
    values_in = qkv[:, 2 * width :].astype(jnp.bfloat16)
    for at in range(0, width, pair):
        cut = slice(at, at + pair)
        out_ref[0, :, cut] = attend_pair(
            queries[:, cut], keys_in[:, cut], values_in[:, cut], None, head_size
        ).astype(jnp.bfloat16)


def group_kernel(x_ref, w_ref, row_ref, col_ref, out_ref, *, head_size):
    sources, _, ser_local, depth = x_ref.shape
    members = w_ref.shape[0]
    width = w_ref.shape[2] // 4
    pair = 2 * head_size
    scale = head_size ** (-0.5)
    rows = x_ref[...].reshape(sources * ser_local, depth)
    bias = jnp.where(row_ref[...] == col_ref[...], 0.0, -1e30).astype(jnp.float32)
    for member in range(members):
        made = jnp.dot(rows, w_ref[member], preferred_element_type=jnp.float32)
        queries = (made[:, :width].astype(jnp.bfloat16) * scale).astype(jnp.bfloat16)
        keys_in = made[:, width : 2 * width].astype(jnp.bfloat16)
        values_in = made[:, 2 * width : 3 * width].astype(jnp.bfloat16)
        gate = jax.nn.sigmoid(made[:, 3 * width :])
        for at in range(0, width, pair):
            cut = slice(at, at + pair)
            got = attend_pair(queries[:, cut], keys_in[:, cut], values_in[:, cut], bias, head_size)
            got = (gate[:, cut] * got).astype(jnp.bfloat16)
            to = member * width + at
            out_ref[:, 0, :, to : to + pair] = got.reshape(sources, ser_local, pair)


def join_kernel(group_ref, own_ref, other_ref, w_ref, keep_ref, send_ref):
    me = lax.axis_index("mp")
    block, ser_local, width = group_ref.shape
    half = width // 2
    group = jnp.swapaxes(group_ref[...].astype(jnp.float32), 0, 1).reshape(ser_local * block, width)
    own = own_ref[...].reshape(ser_local * block, half).astype(jnp.float32)
    other = other_ref[...].reshape(ser_local * block, half).astype(jnp.float32)
    is_low = me == 0
    low = jnp.where(is_low, own, other)
    high = jnp.where(is_low, other, own)
    merged = (jnp.concatenate([low, high], axis=1) + group).astype(jnp.bfloat16)
    result = jnp.dot(merged, w_ref[...], preferred_element_type=jnp.float32).astype(jnp.bfloat16)
    result = result.reshape(ser_local, block, width)
    low, high = result[:, :, :half], result[:, :, half:]
    keep_ref[...] = jnp.where(is_low, low, high)
    send_ref[...] = jnp.where(is_low, high, low)


def join_heads(weight):
    depth, heads, triple = weight.shape
    split = weight.reshape(depth, heads, 3, triple // 3)
    return jnp.swapaxes(split, 1, 2).reshape(depth, heads * triple)


def split_patches(series_in, norm_gain, w_time, w_group, w_gate, w_out, group_of):
    ser_local, patches, depth = series_in.shape
    heads_local = w_time.shape[1]
    head_size = w_time.shape[2] // 3
    width = heads_local * head_size
    total = heads_local * head_size * 2
    ns, nm = lax.axis_size("series"), lax.axis_size("mp")
    me = lax.axis_index("mp")
    half = patches // nm
    each = half // ns
    n_series = group_of.shape[0]
    params = lambda: pltpu.CompilerParams(vmem_limit_bytes=VMEM_BYTES)

    own_half = lax.dynamic_slice_in_dim(series_in, me * half, half, 1)
    send = rms_norm(own_half, norm_gain)
    send = jnp.transpose(send.reshape(ser_local, ns, each, depth), (1, 2, 0, 3))

    w_mix = jnp.concatenate([join_heads(w_group), w_gate], axis=1)
    w_mix = lax.all_gather(w_mix, "mp", axis=0)
    w_full = lax.all_gather(w_out, "mp", axis=0, tiled=True)

    step = each // CHUNKS
    received = []
    for c in range(CHUNKS):
        piece = send[:, c * step : (c + 1) * step]
        received.append(lax.all_to_all(piece, "series", split_axis=0, concat_axis=0, tiled=True))

    time_out = pl.pallas_call(
        partial(time_kernel, head_size=head_size),
        grid=(ser_local,),
        in_specs=[
            pl.BlockSpec((1, patches, depth), lambda i: (i, 0, 0)),
            pl.BlockSpec((1, depth), lambda i: (0, 0)),
            pl.BlockSpec((depth, 3 * width), lambda i: (0, 0)),
        ],
        out_specs=pl.BlockSpec((1, patches, width), lambda i: (i, 0, 0)),
        out_shape=jax.ShapeDtypeStruct((ser_local, patches, width), jnp.bfloat16),
        compiler_params=params(),
        name="time_path",
        cost_estimate=pl.CostEstimate(
            flops=2 * ser_local * patches * (depth * 3 * width + 4 * patches * width),
            bytes_accessed=ser_local * patches * (depth + width) * 2,
            transcendentals=ser_local * heads_local * patches * patches,
        ),
    )(series_in, norm_gain.reshape(1, depth), join_heads(w_time))

    swap = [(i, nm - 1 - i) for i in range(nm)]
    time_send = lax.dynamic_slice_in_dim(time_out, (nm - 1 - me) * half, half, 1)
    time_other = lax.ppermute(time_send, "mp", swap)
    time_own = lax.dynamic_slice_in_dim(time_out, me * half, half, 1)

    returned = []
    for c in range(CHUNKS):
        group_out = pl.pallas_call(
            partial(group_kernel, head_size=head_size),
            grid=(step,),
            in_specs=[
                pl.BlockSpec((ns, 1, ser_local, depth), lambda i: (0, i, 0, 0)),
                pl.BlockSpec((nm, depth, 4 * width), lambda i: (0, 0, 0)),
                pl.BlockSpec((n_series, 1), lambda i: (0, 0)),
                pl.BlockSpec((1, n_series), lambda i: (0, 0)),
            ],
            out_specs=pl.BlockSpec((ns, 1, ser_local, total), lambda i: (0, i, 0, 0)),
            out_shape=jax.ShapeDtypeStruct((ns, step, ser_local, total), jnp.bfloat16),
            compiler_params=params(),
            name="group_path",
            cost_estimate=pl.CostEstimate(
                flops=2 * step * n_series * (depth * 4 * total + 4 * n_series * total),
                bytes_accessed=step * n_series * (depth + total) * 2,
                transcendentals=step * nm * heads_local * n_series * n_series,
            ),
        )(received[c], w_mix, group_of.reshape(n_series, 1), group_of.reshape(1, n_series))
        returned.append(
            lax.all_to_all(group_out, "series", split_axis=0, concat_axis=0, tiled=True)
        )

    back = jnp.concatenate(returned, axis=1) if CHUNKS > 1 else returned[0]
    back = back.reshape(half, ser_local, total)
    block = 16
    keep, give = pl.pallas_call(
        join_kernel,
        grid=(half // block,),
        in_specs=[
            pl.BlockSpec((block, ser_local, total), lambda i: (i, 0, 0)),
            pl.BlockSpec((ser_local, block, width), lambda i: (0, i, 0)),
            pl.BlockSpec((ser_local, block, width), lambda i: (0, i, 0)),
            pl.BlockSpec((total, total), lambda i: (0, 0)),
        ],
        out_specs=[pl.BlockSpec((ser_local, block, width), lambda i: (0, i, 0))] * 2,
        out_shape=[jax.ShapeDtypeStruct((ser_local, half, width), jnp.bfloat16)] * 2,
        compiler_params=params(),
        name="join_path",
    )(back, time_own, time_other, w_full)
    taken = lax.ppermute(give, "mp", swap)
    is_low = me == 0
    return jnp.concatenate(
        [jnp.where(is_low, keep, taken), jnp.where(is_low, taken, keep)], axis=1
    )


def time_attend(time_qkv):
    head_size = time_qkv.shape[-1]
    queries = time_qkv[:, :, :, 0]
    keys_in = time_qkv[:, :, :, 1]
    values_in = time_qkv[:, :, :, 2]
    scores = jnp.einsum(
        "bphd,bqhd->bhpq", queries, keys_in, preferred_element_type=jnp.float32
    ) * head_size ** (-0.5)
    weights = jax.nn.softmax(scores, axis=-1).astype(jnp.bfloat16)
    return jnp.einsum(
        "bhpq,bqhd->bphd", weights, values_in, preferred_element_type=jnp.float32
    ).astype(jnp.bfloat16)


def group_patch(patch_qkv, same_group):
    head_size = patch_qkv.shape[-1]
    queries = patch_qkv[:, :, 0]
    keys_in = patch_qkv[:, :, 1]
    values_in = patch_qkv[:, :, 2]
    scores = jnp.einsum(
        "ihd,jhd->hij", queries, keys_in, preferred_element_type=jnp.float32
    ) * head_size ** (-0.5)
    scores = jnp.where(same_group[None], scores, -1e30)
    weights = jax.nn.softmax(scores, axis=-1).astype(jnp.bfloat16)
    return jnp.einsum(
        "hij,jhd->ihd", weights, values_in, preferred_element_type=jnp.float32
    ).astype(jnp.bfloat16)


def split_heads(series_in, norm_gain, w_time, w_group, w_gate, w_out, group_of):
    ser_local, patches, width = series_in.shape
    heads_local = w_time.shape[1]
    head_size = w_time.shape[2] // 3
    normed = rms_norm(series_in, norm_gain)
    flat_rows = normed.reshape(ser_local * patches, width)
    time_qkv = jnp.dot(
        flat_rows, w_time.reshape(width, -1), preferred_element_type=jnp.float32
    ).astype(jnp.bfloat16)
    time_qkv = time_qkv.reshape(ser_local, patches, heads_local, 3, head_size)
    time_out = time_attend(time_qkv).reshape(ser_local * patches, heads_local * head_size)
    quarter = width // lax.axis_size("mp")
    own_columns = lax.dynamic_slice_in_dim(normed, lax.axis_index("mp") * quarter, quarter, 2)
    moved = lax.all_to_all(own_columns, "series", split_axis=1, concat_axis=0, tiled=True)
    full_rows = lax.all_gather(moved, "mp", axis=2, tiled=True)
    owned = jnp.dot(
        full_rows.reshape(-1, width), w_group.reshape(width, -1), preferred_element_type=jnp.float32
    ).astype(jnp.bfloat16)
    owned = owned.reshape(full_rows.shape[0], full_rows.shape[1], -1)
    all_series, patch_local = (owned.shape[0], owned.shape[1])
    owned = owned.reshape(all_series, patch_local, heads_local, 3, head_size)
    same_group = group_of[:, None] == group_of[None, :]
    group_out = lax.map(partial(group_patch, same_group=same_group), jnp.moveaxis(owned, 1, 0))
    group_out = jnp.moveaxis(group_out, 0, 1).reshape(
        all_series, patch_local, heads_local * head_size
    )
    returned = lax.all_to_all(group_out, "series", split_axis=0, concat_axis=1, tiled=True)
    returned = returned.reshape(ser_local * patches, heads_local * head_size)
    gate_value = jax.nn.sigmoid(jnp.dot(flat_rows, w_gate, preferred_element_type=jnp.float32))
    merged = (time_out.astype(jnp.float32) + gate_value * returned.astype(jnp.float32)).astype(
        jnp.bfloat16
    )
    head_term = jnp.dot(merged, w_out, preferred_element_type=jnp.float32).reshape(
        ser_local, patches, width
    )
    return lax.psum_scatter(head_term.astype(jnp.bfloat16), "mp", scatter_dimension=2, tiled=True)


def per_device(series_in, norm_gain, w_time, *rest):
    ser_local, patches, _ = series_in.shape
    ns, nm = lax.axis_size("series"), lax.axis_size("mp")
    pairs = w_time.shape[1] % 2 == 0 and (2 * w_time.shape[2] // 3) % 128 == 0
    tiled = ser_local % 16 == 0 and patches % (ns * nm * CHUNKS) == 0 and patches // nm % 16 == 0
    if nm == 2 and pairs and tiled:
        return split_patches(series_in, norm_gain, w_time, *rest)
    return split_heads(series_in, norm_gain, w_time, *rest)


def solution(mesh):
    placed = (
        P("series", None, None),
        P(),
        P(None, "mp", None),
        P(None, "mp", None),
        P(None, "mp"),
        P("mp", None),
        P(),
    )
    return jax.shard_map(
        per_device, mesh=mesh, in_specs=placed, out_specs=P("series", None, "mp"), check_vma=False
    )
```

```python
from functools import partial

import jax
import jax.numpy as jnp
from jax import lax
from jax.experimental import pallas as pl
from jax.experimental.pallas import tpu as pltpu
from jax.sharding import PartitionSpec as P


CHUNKS = 2
VMEM_BYTES = 60 * 1024 * 1024


def rms_norm(series_in, norm_gain):
    values_f = series_in.astype(jnp.float32)
    mean_sq = jnp.mean(values_f * values_f, axis=-1, keepdims=True)
    return (values_f * lax.rsqrt(mean_sq + 1e-06) * norm_gain).astype(jnp.bfloat16)


def attend_pair(queries, keys_in, values_in, bias, head_size):
    lane = lax.broadcasted_iota(jnp.int32, queries.shape, 1)
    first = lane < head_size
    zero = jnp.zeros_like(queries)
    ones = jnp.ones_like(values_in)
    extended = jnp.concatenate([values_in, ones], axis=1)
    outs = []
    for own in (jnp.where(first, queries, zero), jnp.where(first, zero, queries)):
        scores = lax.dot_general(
            own, keys_in, (((1,), (1,)), ((), ())), preferred_element_type=jnp.float32
        )
        if bias is not None:
            scores = scores + bias
        top = jnp.max(scores, axis=1, keepdims=True)
        weights = jnp.exp(scores - top).astype(jnp.bfloat16)
        outs.append(jnp.dot(weights, extended, preferred_element_type=jnp.float32))
    pair = values_in.shape[1]
    sums = jnp.where(first, outs[0][:, pair:], outs[1][:, pair:])
    tops = jnp.where(first, outs[0][:, :pair], outs[1][:, :pair])
    return tops / sums


def fill_heads(made_ref, at, part, first_head, head_size, width):
    for head in range(part.shape[0]):
        for kind in range(3):
            to = kind * width + (first_head + head) * head_size
            if not isinstance(to, int):
                to = pl.multiple_of(to, head_size)
            rows = part[head, kind * head_size : (kind + 1) * head_size]
            made_ref[at, pl.ds(to, head_size)] = rows


def project(rows, weight):
    return lax.dot_general(
        rows, weight, (((1,), (1,)), ((), ())), preferred_element_type=jnp.float32
    )


def prep_kernel(_, x_ref, gain_ref, *rest):
    out_ref = rest[-1]
    normed = rms_norm(x_ref[...], gain_ref[...].reshape(1, 1, -1)).astype(jnp.float32)
    out_ref[...] = jnp.swapaxes(normed, 0, 1).astype(jnp.bfloat16)


def time_kernel(x_ref, gain_ref, w_ref, _, own_ref, give_ref, made_ref, *, head_size):
    is_low = lax.axis_index("mp") == 0
    width = own_ref.shape[-1]
    half = own_ref.shape[1]

    @pl.when(pl.program_id(0) == 0)
    def _():
        fill_heads(made_ref, 0, w_ref, 0, head_size, width)

    normed = rms_norm(x_ref[0], gain_ref[...])
    pair = 2 * head_size
    scale = head_size ** (-0.5)
    qkv = project(normed, made_ref[0])
    queries = (qkv[:, :width].astype(jnp.bfloat16) * scale).astype(jnp.bfloat16)
    keys_in = qkv[:, width : 2 * width].astype(jnp.bfloat16)
    values_in = qkv[:, 2 * width :].astype(jnp.bfloat16)
    for at in range(0, width, pair):
        cut = slice(at, at + pair)
        got = attend_pair(
            queries[:, cut], keys_in[:, cut], values_in[:, cut], None, head_size
        )
        low, high = got[:half], got[half:]
        own_ref[0, :, cut] = jnp.where(is_low, low, high).astype(jnp.bfloat16)
        give_ref[0, :, cut] = jnp.where(is_low, high, low).astype(jnp.bfloat16)


def group_kernel(
    x_ref, w_ref, wa_ref, wb_ref, g_ref, ga_ref, gb_ref, row_ref, col_ref, _, out_ref,
    made_ref, gate_ref, *, head_size
):
    me = lax.axis_index("mp")
    core = lax.axis_index("series") % 2
    sources, _, ser_local, depth = x_ref.shape
    width = g_ref.shape[1]
    half_heads = wa_ref.shape[0]
    half_depth = ga_ref.shape[0]

    @pl.when(pl.program_id(0) == 0)
    def _():
        fill_heads(made_ref, me, w_ref, 0, head_size, width)
        fill_heads(made_ref, 1 - me, wa_ref, core * half_heads, head_size, width)
        fill_heads(made_ref, 1 - me, wb_ref, (1 - core) * half_heads, head_size, width)
        gate_ref[me] = g_ref[...]
        for part, at in ((ga_ref, core), (gb_ref, 1 - core)):
            to = pl.multiple_of(at * half_depth, half_depth)
            gate_ref[1 - me, pl.ds(to, half_depth)] = part[...]

    pair = 2 * head_size
    scale = head_size ** (-0.5)
    rows = x_ref[...].reshape(sources * ser_local, depth)
    bias = jnp.where(row_ref[...] == col_ref[...], 0.0, -1e30).astype(jnp.float32)
    for member in range(2):
        made = project(rows, made_ref[member])
        queries = (made[:, :width].astype(jnp.bfloat16) * scale).astype(jnp.bfloat16)
        keys_in = made[:, width : 2 * width].astype(jnp.bfloat16)
        values_in = made[:, 2 * width :].astype(jnp.bfloat16)
        gate = jax.nn.sigmoid(jnp.dot(rows, gate_ref[member], preferred_element_type=jnp.float32))
        for at in range(0, width, pair):
            cut = slice(at, at + pair)
            got = attend_pair(queries[:, cut], keys_in[:, cut], values_in[:, cut], bias, head_size)
            got = (gate[:, cut] * got).astype(jnp.bfloat16)
            to = member * width + at
            out_ref[:, 0, :, to : to + pair] = got.reshape(sources, ser_local, pair)


def join_kernel(group_ref, own_ref, other_ref, w_ref, wa_ref, wb_ref, keep_ref, send_ref, full_ref):
    me = lax.axis_index("mp")
    core = lax.axis_index("series") % 2
    block, ser_local, width = group_ref.shape
    half = width // 2
    quarter = half // 2

    @pl.when(pl.program_id(0) == 0)
    def _():
        full_ref[pl.ds(pl.multiple_of(me * half, half), half)] = w_ref[...]
        for part, at in ((wa_ref, core), (wb_ref, 1 - core)):
            to = pl.multiple_of((1 - me) * half + at * quarter, quarter)
            full_ref[pl.ds(to, quarter)] = part[...]

    group = jnp.swapaxes(group_ref[...].astype(jnp.float32), 0, 1).reshape(ser_local * block, width)
    own = own_ref[...].reshape(ser_local * block, half).astype(jnp.float32)
    other = other_ref[...].reshape(ser_local * block, half).astype(jnp.float32)
    is_low = me == 0
    low = jnp.where(is_low, own, other)
    high = jnp.where(is_low, other, own)
    merged = (jnp.concatenate([low, high], axis=1) + group).astype(jnp.bfloat16)
    result = jnp.dot(merged, full_ref[...], preferred_element_type=jnp.float32).astype(jnp.bfloat16)
    result = result.reshape(ser_local, block, width)
    low, high = result[:, :, :half], result[:, :, half:]
    keep_ref[...] = jnp.where(is_low, low, high)
    send_ref[...] = jnp.where(is_low, high, low)


def split_patches(series_in, norm_gain, w_time, w_group, w_gate, w_out, group_of):
    ser_local, patches, depth = series_in.shape
    heads_local = w_time.shape[1]
    head_size = w_time.shape[2] // 3
    width = heads_local * head_size
    ns, nm = lax.axis_size("series"), lax.axis_size("mp")
    total = width * nm
    me = lax.axis_index("mp")
    core = lax.axis_index("series") % 2
    half = patches // nm
    each = half // ns
    n_series = group_of.shape[0]
    params = lambda: pltpu.CompilerParams(vmem_limit_bytes=VMEM_BYTES)
    whole = lambda *shape: pl.BlockSpec(shape, lambda *i: (0,) * len(shape))
    unread = pl.BlockSpec(memory_space=pl.ANY)
    swap = [(i, nm - 1 - i) for i in range(nm)]
    sibling = [(i, i ^ 1) for i in range(ns)]

    def from_partner(weight):
        rows = weight.shape[0] // 2
        part = lax.dynamic_slice_in_dim(weight, core * rows, rows, 0)
        first = lax.ppermute(part, "mp", swap)
        return first, lax.ppermute(first, "series", sibling)

    step = each // CHUNKS
    block = 16
    gain = norm_gain.reshape(1, depth)
    me_ref = me.astype(jnp.int32).reshape(1)
    sent, received = [], []
    chunk = ns * step

    def send_chunk(c, after):
        piece = pl.pallas_call(
            prep_kernel,
            grid_spec=pltpu.PrefetchScalarGridSpec(
                num_scalar_prefetch=1,
                grid=(chunk // block,),
                in_specs=[
                    pl.BlockSpec(
                        (ser_local, block, depth),
                        lambda i, m, c=c: (0, (m[0] * half + c * chunk) // block + i, 0),
                    ),
                    whole(1, depth),
                    *[unread] * len(after),
                ],
                out_specs=pl.BlockSpec((block, ser_local, depth), lambda i, m: (i, 0, 0)),
            ),
            out_shape=jax.ShapeDtypeStruct((chunk, ser_local, depth), jnp.bfloat16),
            compiler_params=params(),
            name="prep_path",
        )(me_ref, series_in, gain, *after)
        sent.append(piece)
        received.append(
            lax.all_to_all(
                piece.reshape(ns, step, ser_local, depth),
                "series", split_axis=0, concat_axis=0, tiled=True,
            )
        )

    send_chunk(0, ())

    turned = lambda weight: jnp.transpose(weight, (1, 2, 0))
    group_own = turned(w_group)
    group_a, group_b = from_partner(group_own)
    gate_a, gate_b = from_partner(w_gate)
    out_a, out_b = from_partner(w_out)

    time_own, time_give = pl.pallas_call(
        partial(time_kernel, head_size=head_size),
        grid=(ser_local,),
        in_specs=[
            pl.BlockSpec((1, patches, depth), lambda i: (i, 0, 0)),
            whole(1, depth),
            whole(heads_local, 3 * head_size, depth),
            unread,
        ],
        out_specs=[pl.BlockSpec((1, half, width), lambda i: (i, 0, 0))] * 2,
        out_shape=[jax.ShapeDtypeStruct((ser_local, half, width), jnp.bfloat16)] * 2,
        scratch_shapes=[pltpu.VMEM((1, 3 * width, depth), jnp.bfloat16)],
        compiler_params=params(),
        name="time_path",
        cost_estimate=pl.CostEstimate(
            flops=2 * ser_local * patches * (depth * 3 * width + 4 * patches * width),
            bytes_accessed=ser_local * patches * (depth + width) * 2,
            transcendentals=ser_local * heads_local * patches * patches,
        ),
    )(series_in, gain, turned(w_time), sent[0])
    for c in range(1, CHUNKS):
        send_chunk(c, (time_own, group_a, gate_a, out_a) if c == 1 else (sent[-1],))

    time_other = lax.ppermute(time_give, "mp", swap)

    out = jnp.zeros((ser_local, patches, width), jnp.bfloat16)
    last = time_own
    backs = []
    for c in range(CHUNKS):
        call = pl.pallas_call(
            partial(group_kernel, head_size=head_size),
            grid=(step,),
            in_specs=[
                pl.BlockSpec((ns, 1, ser_local, depth), lambda i: (0, i, 0, 0)),
                whole(*group_own.shape),
                whole(*group_a.shape),
                whole(*group_b.shape),
                whole(*w_gate.shape),
                whole(*gate_a.shape),
                whole(*gate_b.shape),
                whole(n_series, 1),
                whole(1, n_series),
                unread,
            ],
            out_specs=pl.BlockSpec((ns, 1, ser_local, total), lambda i: (0, i, 0, 0)),
            out_shape=jax.ShapeDtypeStruct((ns, step, ser_local, total), jnp.bfloat16),
            scratch_shapes=[
                pltpu.VMEM((nm, 3 * width, depth), jnp.bfloat16),
                pltpu.VMEM((nm, depth, width), jnp.bfloat16),
            ],
            compiler_params=params(),
            name="group_path",
            cost_estimate=pl.CostEstimate(
                flops=2 * step * n_series * (depth * 4 * total + 4 * n_series * total),
                bytes_accessed=step * n_series * (depth + total) * 2,
                transcendentals=step * nm * heads_local * n_series * n_series,
            ),
        )
        group_out = call(
        received[c], group_own, group_a, group_b, w_gate, gate_a, gate_b,
        group_of.reshape(n_series, 1), group_of.reshape(1, n_series), last,
        )
        last = group_out
        backs.append(
            lax.all_to_all(group_out, "series", split_axis=0, concat_axis=0, tiled=True)
        )

    for c in range(CHUNKS):
        back = backs[c].reshape(chunk, ser_local, total)
        at_chunk = lambda i, c=c: (0, c * chunk // block + i, 0)
        keep, give = pl.pallas_call(
            join_kernel,
            grid=(chunk // block,),
            in_specs=[
                pl.BlockSpec((block, ser_local, total), lambda i: (i, 0, 0)),
                pl.BlockSpec((ser_local, block, width), at_chunk),
                pl.BlockSpec((ser_local, block, width), at_chunk),
                whole(*w_out.shape),
                whole(*out_a.shape),
                whole(*out_b.shape),
            ],
            out_specs=[pl.BlockSpec((ser_local, block, width), lambda i: (0, i, 0))] * 2,
            out_shape=[jax.ShapeDtypeStruct((ser_local, chunk, width), jnp.bfloat16)] * 2,
            scratch_shapes=[pltpu.VMEM((total, total), jnp.bfloat16)],
            compiler_params=params(),
            name="join_path",
            cost_estimate=pl.CostEstimate(
                flops=2 * chunk * ser_local * total * total,
                bytes_accessed=4 * chunk * ser_local * total * 2,
                transcendentals=0,
            ),
        )(back, time_own, time_other, w_out, out_a, out_b)
        taken = lax.ppermute(give, "mp", swap)
        out = lax.dynamic_update_slice_in_dim(out, keep, me * half + c * chunk, 1)
        out = lax.dynamic_update_slice_in_dim(out, taken, (nm - 1 - me) * half + c * chunk, 1)
    return out


def time_attend(time_qkv):
    head_size = time_qkv.shape[-1]
    queries = time_qkv[:, :, :, 0]
    keys_in = time_qkv[:, :, :, 1]
    values_in = time_qkv[:, :, :, 2]
    scores = jnp.einsum(
        "bphd,bqhd->bhpq", queries, keys_in, preferred_element_type=jnp.float32
    ) * head_size ** (-0.5)
    weights = jax.nn.softmax(scores, axis=-1).astype(jnp.bfloat16)
    return jnp.einsum(
        "bhpq,bqhd->bphd", weights, values_in, preferred_element_type=jnp.float32
    ).astype(jnp.bfloat16)


def group_patch(patch_qkv, same_group):
    head_size = patch_qkv.shape[-1]
    queries = patch_qkv[:, :, 0]
    keys_in = patch_qkv[:, :, 1]
    values_in = patch_qkv[:, :, 2]
    scores = jnp.einsum(
        "ihd,jhd->hij", queries, keys_in, preferred_element_type=jnp.float32
    ) * head_size ** (-0.5)
    scores = jnp.where(same_group[None], scores, -1e30)
    weights = jax.nn.softmax(scores, axis=-1).astype(jnp.bfloat16)
    return jnp.einsum(
        "hij,jhd->ihd", weights, values_in, preferred_element_type=jnp.float32
    ).astype(jnp.bfloat16)


def split_heads(series_in, norm_gain, w_time, w_group, w_gate, w_out, group_of):
    ser_local, patches, width = series_in.shape
    heads_local = w_time.shape[1]
    head_size = w_time.shape[2] // 3
    normed = rms_norm(series_in, norm_gain)
    flat_rows = normed.reshape(ser_local * patches, width)
    time_qkv = jnp.dot(
        flat_rows, w_time.reshape(width, -1), preferred_element_type=jnp.float32
    ).astype(jnp.bfloat16)
    time_qkv = time_qkv.reshape(ser_local, patches, heads_local, 3, head_size)
    time_out = time_attend(time_qkv).reshape(ser_local * patches, heads_local * head_size)
    quarter = width // lax.axis_size("mp")
    own_columns = lax.dynamic_slice_in_dim(normed, lax.axis_index("mp") * quarter, quarter, 2)
    moved = lax.all_to_all(own_columns, "series", split_axis=1, concat_axis=0, tiled=True)
    full_rows = lax.all_gather(moved, "mp", axis=2, tiled=True)
    owned = jnp.dot(
        full_rows.reshape(-1, width), w_group.reshape(width, -1), preferred_element_type=jnp.float32
    ).astype(jnp.bfloat16)
    owned = owned.reshape(full_rows.shape[0], full_rows.shape[1], -1)
    all_series, patch_local = (owned.shape[0], owned.shape[1])
    owned = owned.reshape(all_series, patch_local, heads_local, 3, head_size)
    same_group = group_of[:, None] == group_of[None, :]
    group_out = lax.map(partial(group_patch, same_group=same_group), jnp.moveaxis(owned, 1, 0))
    group_out = jnp.moveaxis(group_out, 0, 1).reshape(
        all_series, patch_local, heads_local * head_size
    )
    returned = lax.all_to_all(group_out, "series", split_axis=0, concat_axis=1, tiled=True)
    returned = returned.reshape(ser_local * patches, heads_local * head_size)
    gate_value = jax.nn.sigmoid(jnp.dot(flat_rows, w_gate, preferred_element_type=jnp.float32))
    merged = (time_out.astype(jnp.float32) + gate_value * returned.astype(jnp.float32)).astype(
        jnp.bfloat16
    )
    head_term = jnp.dot(merged, w_out, preferred_element_type=jnp.float32).reshape(
        ser_local, patches, width
    )
    return lax.psum_scatter(head_term.astype(jnp.bfloat16), "mp", scatter_dimension=2, tiled=True)


def per_device(series_in, norm_gain, w_time, *rest):
    ser_local, patches, _ = series_in.shape
    ns, nm = lax.axis_size("series"), lax.axis_size("mp")
    pairs = w_time.shape[1] % 2 == 0 and w_time.shape[2] % 48 == 0 and (2 * w_time.shape[2] // 3) % 128 == 0
    tiled = ser_local % 16 == 0 and patches % (ns * nm * CHUNKS) == 0 and patches // nm % (16 * CHUNKS) == 0
    tiled = tiled and ns % 2 == 0 and w_time.shape[0] % 32 == 0
    if nm == 2 and pairs and tiled:
        return split_patches(series_in, norm_gain, w_time, *rest)
    return split_heads(series_in, norm_gain, w_time, *rest)


def solution(mesh):
    placed = (
        P("series", None, None),
        P(),
        P(None, "mp", None),
        P(None, "mp", None),
        P(None, "mp"),
        P("mp", None),
        P(),
    )
    return jax.shard_map(
        per_device, mesh=mesh, in_specs=placed, out_specs=P("series", None, "mp"), check_vma=False
    )
```

```python
from functools import partial

import jax
import jax.numpy as jnp
from jax import lax
from jax.experimental import pallas as pl
from jax.experimental.pallas import tpu as pltpu
from jax.sharding import PartitionSpec as P


SHARES = (3, 3, 2)
FIRST_SERIES = (3, 8)
VMEM_BYTES = 60 * 1024 * 1024


def rms_norm(series_in, norm_gain):
    values_f = series_in.astype(jnp.float32)
    mean_sq = jnp.mean(values_f * values_f, axis=-1, keepdims=True)
    return (values_f * lax.rsqrt(mean_sq + 1e-06) * norm_gain).astype(jnp.bfloat16)


def attend_pair(queries, keys_in, values_in, bias, head_size):
    lane = lax.broadcasted_iota(jnp.int32, queries.shape, 1)
    first = lane < head_size
    zero = jnp.zeros_like(queries)
    ones = jnp.ones_like(values_in)
    extended = jnp.concatenate([values_in, ones], axis=1)
    outs = []
    for own in (jnp.where(first, queries, zero), jnp.where(first, zero, queries)):
        scores = lax.dot_general(
            own, keys_in, (((1,), (1,)), ((), ())), preferred_element_type=jnp.float32
        )
        if bias is not None:
            scores = scores + bias
        top = jnp.max(scores, axis=1, keepdims=True)
        weights = jnp.exp(scores - top).astype(jnp.bfloat16)
        outs.append(jnp.dot(weights, extended, preferred_element_type=jnp.float32))
    pair = values_in.shape[1]
    sums = jnp.where(first, outs[0][:, pair:], outs[1][:, pair:])
    tops = jnp.where(first, outs[0][:, :pair], outs[1][:, :pair])
    return tops / sums


def fill_heads(made_ref, at, part, first_head, head_size, width):
    for head in range(part.shape[0]):
        for kind in range(3):
            to = kind * width + (first_head + head) * head_size
            if not isinstance(to, int):
                to = pl.multiple_of(to, head_size)
            rows = part[head, kind * head_size : (kind + 1) * head_size]
            made_ref[at, pl.ds(to, head_size)] = rows


def project(rows, weight):
    return lax.dot_general(
        rows, weight, (((1,), (1,)), ((), ())), preferred_element_type=jnp.float32
    )


def prep_kernel(_, x_ref, gain_ref, *rest):
    out_ref = rest[-1]
    normed = rms_norm(x_ref[...], gain_ref[...]).astype(jnp.float32)
    out_ref[...] = jnp.swapaxes(normed, 0, 1).astype(jnp.bfloat16)


def time_kernel(x_ref, gain_ref, w_ref, *rest, head_size):
    own_ref, give_ref, made_ref = rest[-3:]
    is_low = lax.axis_index("mp") == 0
    width = own_ref.shape[-1]
    half = own_ref.shape[1]

    @pl.when(pl.program_id(0) == 0)
    def _():
        fill_heads(made_ref, 0, w_ref, 0, head_size, width)

    normed = rms_norm(x_ref[0], gain_ref[...])
    pair = 2 * head_size
    scale = head_size ** (-0.5)
    qkv = project(normed, made_ref[0])
    queries = (qkv[:, :width].astype(jnp.bfloat16) * scale).astype(jnp.bfloat16)
    keys_in = qkv[:, width : 2 * width].astype(jnp.bfloat16)
    values_in = qkv[:, 2 * width :].astype(jnp.bfloat16)
    for at in range(0, width, pair):
        cut = slice(at, at + pair)
        got = attend_pair(
            queries[:, cut], keys_in[:, cut], values_in[:, cut], None, head_size
        )
        low, high = got[:half], got[half:]
        own_ref[0, :, cut] = jnp.where(is_low, low, high).astype(jnp.bfloat16)
        give_ref[0, :, cut] = jnp.where(is_low, high, low).astype(jnp.bfloat16)


def group_kernel(
    x_ref, w_ref, wa_ref, wb_ref, g_ref, ga_ref, gb_ref, row_ref, col_ref, _, out_ref,
    made_ref, gate_ref, *, head_size
):
    me = lax.axis_index("mp")
    core = lax.axis_index("series") % 2
    sources, _, ser_local, depth = x_ref.shape
    width = g_ref.shape[1]
    half_heads = wa_ref.shape[0]
    half_depth = ga_ref.shape[0]

    @pl.when(pl.program_id(0) == 0)
    def _():
        fill_heads(made_ref, me, w_ref, 0, head_size, width)
        fill_heads(made_ref, 1 - me, wa_ref, core * half_heads, head_size, width)
        fill_heads(made_ref, 1 - me, wb_ref, (1 - core) * half_heads, head_size, width)
        gate_ref[me] = g_ref[...]
        for part, at in ((ga_ref, core), (gb_ref, 1 - core)):
            to = pl.multiple_of(at * half_depth, half_depth)
            gate_ref[1 - me, pl.ds(to, half_depth)] = part[...]

    pair = 2 * head_size
    scale = head_size ** (-0.5)
    rows = x_ref[...].reshape(sources * ser_local, depth)
    bias = jnp.where(row_ref[...] == col_ref[...], 0.0, -1e30).astype(jnp.float32)
    for member in range(2):
        made = project(rows, made_ref[member])
        queries = (made[:, :width].astype(jnp.bfloat16) * scale).astype(jnp.bfloat16)
        keys_in = made[:, width : 2 * width].astype(jnp.bfloat16)
        values_in = made[:, 2 * width :].astype(jnp.bfloat16)
        gate = jax.nn.sigmoid(jnp.dot(rows, gate_ref[member], preferred_element_type=jnp.float32))
        for at in range(0, width, pair):
            cut = slice(at, at + pair)
            got = attend_pair(queries[:, cut], keys_in[:, cut], values_in[:, cut], bias, head_size)
            got = (gate[:, cut] * got).astype(jnp.bfloat16)
            to = member * width + at
            out_ref[:, 0, :, to : to + pair] = got.reshape(sources, ser_local, pair)


def join_kernel(group_ref, own_a, own_b, other_a, other_b, w_ref, wa_ref, wb_ref, keep_ref, send_ref, full_ref):
    me = lax.axis_index("mp")
    core = lax.axis_index("series") % 2
    block, ser_local, width = group_ref.shape
    half = width // 2
    quarter = half // 2

    @pl.when(pl.program_id(0) == 0)
    def _():
        full_ref[pl.ds(pl.multiple_of(me * half, half), half)] = w_ref[...]
        for part, at in ((wa_ref, core), (wb_ref, 1 - core)):
            to = pl.multiple_of((1 - me) * half + at * quarter, quarter)
            full_ref[pl.ds(to, quarter)] = part[...]

    group = jnp.swapaxes(group_ref[...].astype(jnp.float32), 0, 1).reshape(ser_local * block, width)
    own = jnp.concatenate([own_a[...], own_b[...]], axis=0).reshape(ser_local * block, half).astype(jnp.float32)
    other = jnp.concatenate([other_a[...], other_b[...]], axis=0).reshape(ser_local * block, half).astype(jnp.float32)
    is_low = me == 0
    low = jnp.where(is_low, own, other)
    high = jnp.where(is_low, other, own)
    merged = (jnp.concatenate([low, high], axis=1) + group).astype(jnp.bfloat16)
    result = jnp.dot(merged, full_ref[...], preferred_element_type=jnp.float32).astype(jnp.bfloat16)
    result = result.reshape(ser_local, block, width)
    low, high = result[:, :, :half], result[:, :, half:]
    keep_ref[...] = jnp.where(is_low, low, high)
    send_ref[...] = jnp.where(is_low, high, low)


def split_patches(series_in, norm_gain, w_time, w_group, w_gate, w_out, group_of):
    ser_local, patches, depth = series_in.shape
    heads_local = w_time.shape[1]
    head_size = w_time.shape[2] // 3
    width = heads_local * head_size
    ns, nm = lax.axis_size("series"), lax.axis_size("mp")
    total = width * nm
    me = lax.axis_index("mp")
    core = lax.axis_index("series") % 2
    half = patches // nm
    each = half // ns
    n_series = group_of.shape[0]
    params = lambda: pltpu.CompilerParams(vmem_limit_bytes=VMEM_BYTES)
    whole = lambda *shape: pl.BlockSpec(shape, lambda *i: (0,) * len(shape))
    unread = pl.BlockSpec(memory_space=pl.ANY)
    swap = [(i, nm - 1 - i) for i in range(nm)]
    sibling = [(i, i ^ 1) for i in range(ns)]

    def from_partner(weight):
        rows = weight.shape[0] // 2
        part = lax.dynamic_slice_in_dim(weight, core * rows, rows, 0)
        first = lax.ppermute(part, "mp", swap)
        return first, lax.ppermute(first, "series", sibling)

    steps = [each * share // sum(SHARES) for share in SHARES]
    starts = [ns * sum(steps[:c]) for c in range(len(steps))]
    block = 16
    me_ref = me.astype(jnp.int32).reshape(1)
    sent, received = [], []

    def send_chunk(c, after):
        step, chunk = steps[c], ns * steps[c]
        piece = pl.pallas_call(
            prep_kernel,
            grid_spec=pltpu.PrefetchScalarGridSpec(
                num_scalar_prefetch=1,
                grid=(chunk // block,),
                in_specs=[
                    pl.BlockSpec(
                        (ser_local, block, depth),
                        lambda i, m, c=c: (0, (m[0] * half + starts[c]) // block + i, 0),
                    ),
                    whole(depth),
                    *[unread] * len(after),
                ],
                out_specs=pl.BlockSpec((block, ser_local, depth), lambda i, m: (i, 0, 0)),
            ),
            out_shape=jax.ShapeDtypeStruct((chunk, ser_local, depth), jnp.bfloat16),
            compiler_params=params(),
            name="prep_path",
        )(me_ref, series_in, norm_gain, *after)
        sent.append(piece)
        received.append(
            lax.all_to_all(
                piece.reshape(ns, step, ser_local, depth),
                "series", split_axis=0, concat_axis=0, tiled=True,
            )
        )

    send_chunk(0, ())

    turned = lambda weight: jnp.transpose(weight, (1, 2, 0))
    group_own = turned(w_group)
    group_a, group_b = from_partner(group_own)
    gate_a, gate_b = from_partner(w_gate)
    out_a, out_b = from_partner(w_out)

    first_count = ser_local * FIRST_SERIES[0] // FIRST_SERIES[1]
    time_own, time_other = [], []

    def time_call(at, count, after):
        call = pl.pallas_call(
            partial(time_kernel, head_size=head_size),
            grid=(count,),
            in_specs=[
                pl.BlockSpec((1, patches, depth), lambda i: (at + i, 0, 0)),
                whole(depth),
                whole(heads_local, 3 * head_size, depth),
                *[unread] * len(after),
            ],
            out_specs=[pl.BlockSpec((1, half, width), lambda i: (i, 0, 0))] * 2,
            out_shape=[jax.ShapeDtypeStruct((count, half, width), jnp.bfloat16)] * 2,
            scratch_shapes=[pltpu.VMEM((1, 3 * width, depth), jnp.bfloat16)],
            compiler_params=params(),
            name="time_path",
            cost_estimate=pl.CostEstimate(
                flops=2 * count * patches * (depth * 3 * width + 4 * patches * width),
                bytes_accessed=count * patches * (depth + width) * 2,
                transcendentals=count * heads_local * patches * patches,
            ),
        )
        own, give = call(series_in, norm_gain, turned(w_time), *after)
        time_other.append(lax.ppermute(give, "mp", swap))
        time_own.append(own)

    send_chunk(1, (sent[0],))
    time_call(0, first_count, (sent[1],))
    send_chunk(2, (time_own[0],))
    time_call(first_count, ser_local - first_count, (sent[2], group_a, gate_a, out_a))

    counts = [first_count, ser_local - first_count]
    out = jnp.zeros((ser_local, patches, width), jnp.bfloat16)
    last = time_own[1]
    backs = []
    for c, step in enumerate(steps):
        call = pl.pallas_call(
            partial(group_kernel, head_size=head_size),
            grid=(step,),
            in_specs=[
                pl.BlockSpec((ns, 1, ser_local, depth), lambda i: (0, i, 0, 0)),
                whole(*group_own.shape),
                whole(*group_a.shape),
                whole(*group_b.shape),
                whole(*w_gate.shape),
                whole(*gate_a.shape),
                whole(*gate_b.shape),
                whole(n_series, 1),
                whole(1, n_series),
                unread,
            ],
            out_specs=pl.BlockSpec((ns, 1, ser_local, total), lambda i: (0, i, 0, 0)),
            out_shape=jax.ShapeDtypeStruct((ns, step, ser_local, total), jnp.bfloat16),
            scratch_shapes=[
                pltpu.VMEM((nm, 3 * width, depth), jnp.bfloat16),
                pltpu.VMEM((nm, depth, width), jnp.bfloat16),
            ],
            compiler_params=params(),
            name="group_path",
            cost_estimate=pl.CostEstimate(
                flops=2 * step * n_series * (depth * 4 * total + 4 * n_series * total),
                bytes_accessed=step * n_series * (depth + total) * 2,
                transcendentals=step * nm * heads_local * n_series * n_series,
            ),
        )
        group_out = call(
        received[c], group_own, group_a, group_b, w_gate, gate_a, gate_b,
        group_of.reshape(n_series, 1), group_of.reshape(1, n_series), last,
        )
        last = group_out
        backs.append(lax.all_to_all(group_out, "series", split_axis=0, concat_axis=0, tiled=True))

    for c, step in enumerate(steps):
        chunk = ns * step
        back = backs[c].reshape(chunk, ser_local, total)
        at_chunk = lambda i, c=c: (0, starts[c] // block + i, 0)
        call = pl.pallas_call(
            join_kernel,
            grid=(chunk // block,),
            in_specs=[
                pl.BlockSpec((block, ser_local, total), lambda i: (i, 0, 0)),
                *[pl.BlockSpec((n, block, width), at_chunk) for n in counts * 2],
                whole(*w_out.shape),
                whole(*out_a.shape),
                whole(*out_b.shape),
            ],
            out_specs=[pl.BlockSpec((ser_local, block, width), lambda i: (0, i, 0))] * 2,
            out_shape=[jax.ShapeDtypeStruct((ser_local, chunk, width), jnp.bfloat16)] * 2,
            scratch_shapes=[pltpu.VMEM((total, total), jnp.bfloat16)],
            compiler_params=params(),
            name="join_path",
            cost_estimate=pl.CostEstimate(
                flops=2 * chunk * ser_local * total * total,
                bytes_accessed=4 * chunk * ser_local * total * 2,
                transcendentals=0,
            ),
        )
        keep, give = call(back, *time_own, *time_other, w_out, out_a, out_b)
        taken = lax.ppermute(give, "mp", swap)
        out = lax.dynamic_update_slice_in_dim(out, keep, me * half + starts[c], 1)
        out = lax.dynamic_update_slice_in_dim(out, taken, (nm - 1 - me) * half + starts[c], 1)
    return out


def time_attend(time_qkv):
    head_size = time_qkv.shape[-1]
    queries = time_qkv[:, :, :, 0]
    keys_in = time_qkv[:, :, :, 1]
    values_in = time_qkv[:, :, :, 2]
    scores = jnp.einsum(
        "bphd,bqhd->bhpq", queries, keys_in, preferred_element_type=jnp.float32
    ) * head_size ** (-0.5)
    weights = jax.nn.softmax(scores, axis=-1).astype(jnp.bfloat16)
    return jnp.einsum(
        "bhpq,bqhd->bphd", weights, values_in, preferred_element_type=jnp.float32
    ).astype(jnp.bfloat16)


def group_patch(patch_qkv, same_group):
    head_size = patch_qkv.shape[-1]
    queries = patch_qkv[:, :, 0]
    keys_in = patch_qkv[:, :, 1]
    values_in = patch_qkv[:, :, 2]
    scores = jnp.einsum(
        "ihd,jhd->hij", queries, keys_in, preferred_element_type=jnp.float32
    ) * head_size ** (-0.5)
    scores = jnp.where(same_group[None], scores, -1e30)
    weights = jax.nn.softmax(scores, axis=-1).astype(jnp.bfloat16)
    return jnp.einsum(
        "hij,jhd->ihd", weights, values_in, preferred_element_type=jnp.float32
    ).astype(jnp.bfloat16)


def split_heads(series_in, norm_gain, w_time, w_group, w_gate, w_out, group_of):
    ser_local, patches, width = series_in.shape
    heads_local = w_time.shape[1]
    head_size = w_time.shape[2] // 3
    normed = rms_norm(series_in, norm_gain)
    flat_rows = normed.reshape(ser_local * patches, width)
    time_qkv = jnp.dot(
        flat_rows, w_time.reshape(width, -1), preferred_element_type=jnp.float32
    ).astype(jnp.bfloat16)
    time_qkv = time_qkv.reshape(ser_local, patches, heads_local, 3, head_size)
    time_out = time_attend(time_qkv).reshape(ser_local * patches, heads_local * head_size)
    quarter = width // lax.axis_size("mp")
    own_columns = lax.dynamic_slice_in_dim(normed, lax.axis_index("mp") * quarter, quarter, 2)
    moved = lax.all_to_all(own_columns, "series", split_axis=1, concat_axis=0, tiled=True)
    full_rows = lax.all_gather(moved, "mp", axis=2, tiled=True)
    owned = jnp.dot(
        full_rows.reshape(-1, width), w_group.reshape(width, -1), preferred_element_type=jnp.float32
    ).astype(jnp.bfloat16)
    owned = owned.reshape(full_rows.shape[0], full_rows.shape[1], -1)
    all_series, patch_local = (owned.shape[0], owned.shape[1])
    owned = owned.reshape(all_series, patch_local, heads_local, 3, head_size)
    same_group = group_of[:, None] == group_of[None, :]
    group_out = lax.map(partial(group_patch, same_group=same_group), jnp.moveaxis(owned, 1, 0))
    group_out = jnp.moveaxis(group_out, 0, 1).reshape(
        all_series, patch_local, heads_local * head_size
    )
    returned = lax.all_to_all(group_out, "series", split_axis=0, concat_axis=1, tiled=True)
    returned = returned.reshape(ser_local * patches, heads_local * head_size)
    gate_value = jax.nn.sigmoid(jnp.dot(flat_rows, w_gate, preferred_element_type=jnp.float32))
    merged = (time_out.astype(jnp.float32) + gate_value * returned.astype(jnp.float32)).astype(
        jnp.bfloat16
    )
    head_term = jnp.dot(merged, w_out, preferred_element_type=jnp.float32).reshape(
        ser_local, patches, width
    )
    return lax.psum_scatter(head_term.astype(jnp.bfloat16), "mp", scatter_dimension=2, tiled=True)


def per_device(series_in, norm_gain, w_time, *rest):
    ser_local, patches, _ = series_in.shape
    ns, nm = lax.axis_size("series"), lax.axis_size("mp")
    pairs = w_time.shape[1] % 2 == 0 and w_time.shape[2] % 48 == 0 and (2 * w_time.shape[2] // 3) % 128 == 0
    tiled = ser_local % 16 == 0 and patches % (ns * nm * sum(SHARES)) == 0
    tiled = tiled and ns % 16 == 0 and w_time.shape[0] % 32 == 0
    if nm == 2 and pairs and tiled:
        return split_patches(series_in, norm_gain, w_time, *rest)
    return split_heads(series_in, norm_gain, w_time, *rest)


def solution(mesh):
    placed = (
        P("series", None, None),
        P(),
        P(None, "mp", None),
        P(None, "mp", None),
        P(None, "mp"),
        P("mp", None),
        P(),
    )
    return jax.shard_map(
        per_device, mesh=mesh, in_specs=placed, out_specs=P("series", None, "mp"), check_vma=False
    )
```

```python
from functools import partial

import jax
import jax.numpy as jnp
from jax import lax
from jax.experimental import pallas as pl
from jax.experimental.pallas import tpu as pltpu
from jax.sharding import PartitionSpec as P


SHARES = (5, 3)
VMEM_BYTES = 60 * 1024 * 1024


def rms_norm(series_in, norm_gain):
    values_f = series_in.astype(jnp.float32)
    mean_sq = jnp.mean(values_f * values_f, axis=-1, keepdims=True)
    return (values_f * lax.rsqrt(mean_sq + 1e-06) * norm_gain).astype(jnp.bfloat16)


def attend_pair(queries, keys_in, values_in, bias, head_size):
    lane = lax.broadcasted_iota(jnp.int32, queries.shape, 1)
    first = lane < head_size
    zero = jnp.zeros_like(queries)
    ones = jnp.ones_like(values_in)
    extended = jnp.concatenate([values_in, ones], axis=1)
    outs = []
    for own in (jnp.where(first, queries, zero), jnp.where(first, zero, queries)):
        scores = lax.dot_general(
            own, keys_in, (((1,), (1,)), ((), ())), preferred_element_type=jnp.float32
        )
        if bias is not None:
            scores = scores + bias
        top = jnp.max(scores, axis=1, keepdims=True)
        weights = jnp.exp(scores - top).astype(jnp.bfloat16)
        outs.append(jnp.dot(weights, extended, preferred_element_type=jnp.float32))
    pair = values_in.shape[1]
    sums = jnp.where(first, outs[0][:, pair:], outs[1][:, pair:])
    tops = jnp.where(first, outs[0][:, :pair], outs[1][:, :pair])
    return tops / sums


def fill_heads(made_ref, at, part, first_head, head_size, width):
    for head in range(part.shape[0]):
        for kind in range(3):
            to = kind * width + (first_head + head) * head_size
            if not isinstance(to, int):
                to = pl.multiple_of(to, head_size)
            rows = part[head, kind * head_size : (kind + 1) * head_size]
            made_ref[at, pl.ds(to, head_size)] = rows


def project(rows, weight):
    return lax.dot_general(
        rows, weight, (((1,), (1,)), ((), ())), preferred_element_type=jnp.float32
    )


def prep_kernel(_, x_ref, gain_ref, *rest):
    out_ref = rest[-1]
    normed = rms_norm(x_ref[...], gain_ref[...]).astype(jnp.float32)
    out_ref[...] = jnp.swapaxes(normed, 0, 1).astype(jnp.bfloat16)


def time_kernel(x_ref, gain_ref, w_ref, *rest, head_size):
    own_ref, give_ref, made_ref = rest[-3:]
    is_low = lax.axis_index("mp") == 0
    width = own_ref.shape[-1]
    half = own_ref.shape[1]

    @pl.when(pl.program_id(0) == 0)
    def _():
        fill_heads(made_ref, 0, w_ref, 0, head_size, width)

    normed = rms_norm(x_ref[0], gain_ref[...])
    pair = 2 * head_size
    scale = head_size ** (-0.5)
    qkv = project(normed, made_ref[0])
    queries = (qkv[:, :width].astype(jnp.bfloat16) * scale).astype(jnp.bfloat16)
    keys_in = qkv[:, width : 2 * width].astype(jnp.bfloat16)
    values_in = qkv[:, 2 * width :].astype(jnp.bfloat16)
    for at in range(0, width, pair):
        cut = slice(at, at + pair)
        got = attend_pair(
            queries[:, cut], keys_in[:, cut], values_in[:, cut], None, head_size
        )
        low, high = got[:half], got[half:]
        own_ref[0, :, cut] = jnp.where(is_low, low, high).astype(jnp.bfloat16)
        give_ref[0, :, cut] = jnp.where(is_low, high, low).astype(jnp.bfloat16)


def group_kernel(
    x_ref, w_ref, wa_ref, wb_ref, g_ref, ga_ref, gb_ref, row_ref, col_ref, _, out_ref,
    made_ref, gate_ref, *, head_size
):
    me = lax.axis_index("mp")
    core = lax.axis_index("series") % 2
    sources, _, ser_local, depth = x_ref.shape
    width = g_ref.shape[1]
    half_heads = wa_ref.shape[0]
    half_depth = ga_ref.shape[0]

    @pl.when(pl.program_id(0) == 0)
    def _():
        fill_heads(made_ref, me, w_ref, 0, head_size, width)
        fill_heads(made_ref, 1 - me, wa_ref, core * half_heads, head_size, width)
        fill_heads(made_ref, 1 - me, wb_ref, (1 - core) * half_heads, head_size, width)
        gate_ref[me] = g_ref[...]
        for part, at in ((ga_ref, core), (gb_ref, 1 - core)):
            to = pl.multiple_of(at * half_depth, half_depth)
            gate_ref[1 - me, pl.ds(to, half_depth)] = part[...]

    pair = 2 * head_size
    scale = head_size ** (-0.5)
    rows = x_ref[...].reshape(sources * ser_local, depth)
    bias = jnp.where(row_ref[...] == col_ref[...], 0.0, -1e30).astype(jnp.float32)
    for member in range(2):
        made = project(rows, made_ref[member])
        queries = (made[:, :width].astype(jnp.bfloat16) * scale).astype(jnp.bfloat16)
        keys_in = made[:, width : 2 * width].astype(jnp.bfloat16)
        values_in = made[:, 2 * width :].astype(jnp.bfloat16)
        gate = jax.nn.sigmoid(jnp.dot(rows, gate_ref[member], preferred_element_type=jnp.float32))
        for at in range(0, width, pair):
            cut = slice(at, at + pair)
            got = attend_pair(queries[:, cut], keys_in[:, cut], values_in[:, cut], bias, head_size)
            got = (gate[:, cut] * got).astype(jnp.bfloat16)
            to = member * width + at
            out_ref[:, 0, :, to : to + pair] = got.reshape(sources, ser_local, pair)


def join_kernel(
    group_ref, own_ref, other_ref, w_ref, wa_ref, wb_ref, keep_ref, send_ref, full_ref
):
    me = lax.axis_index("mp")
    core = lax.axis_index("series") % 2
    block, ser_local, width = group_ref.shape
    half = width // 2
    quarter = half // 2

    @pl.when(pl.program_id(0) == 0)
    def _():
        full_ref[pl.ds(pl.multiple_of(me * half, half), half)] = w_ref[...]
        for part, at in ((wa_ref, core), (wb_ref, 1 - core)):
            to = pl.multiple_of((1 - me) * half + at * quarter, quarter)
            full_ref[pl.ds(to, quarter)] = part[...]

    group = jnp.swapaxes(group_ref[...].astype(jnp.float32), 0, 1).reshape(ser_local * block, width)
    own = own_ref[...].reshape(ser_local * block, half).astype(jnp.float32)
    other = other_ref[...].reshape(ser_local * block, half).astype(jnp.float32)
    is_low = me == 0
    low = jnp.where(is_low, own, other)
    high = jnp.where(is_low, other, own)
    merged = (jnp.concatenate([low, high], axis=1) + group).astype(jnp.bfloat16)
    result = jnp.dot(merged, full_ref[...], preferred_element_type=jnp.float32).astype(jnp.bfloat16)
    result = result.reshape(ser_local, block, width)
    low, high = result[:, :, :half], result[:, :, half:]
    keep_ref[...] = jnp.where(is_low, low, high)
    send_ref[...] = jnp.where(is_low, high, low)


def split_patches(series_in, norm_gain, w_time, w_group, w_gate, w_out, group_of):
    ser_local, patches, depth = series_in.shape
    heads_local = w_time.shape[1]
    head_size = w_time.shape[2] // 3
    width = heads_local * head_size
    ns, nm = lax.axis_size("series"), lax.axis_size("mp")
    total = width * nm
    me = lax.axis_index("mp")
    core = lax.axis_index("series") % 2
    half = patches // nm
    each = half // ns
    n_series = group_of.shape[0]
    params = lambda: pltpu.CompilerParams(vmem_limit_bytes=VMEM_BYTES)
    whole = lambda *shape: pl.BlockSpec(shape, lambda *i: (0,) * len(shape))
    unread = pl.BlockSpec(memory_space=pl.ANY)
    swap = [(i, nm - 1 - i) for i in range(nm)]
    sibling = [(i, i ^ 1) for i in range(ns)]

    def from_partner(weight):
        rows = weight.shape[0] // 2
        part = lax.dynamic_slice_in_dim(weight, core * rows, rows, 0)
        first = lax.ppermute(part, "mp", swap)
        return first, lax.ppermute(first, "series", sibling)

    steps = [each * share // sum(SHARES) for share in SHARES]
    starts = [ns * sum(steps[:c]) for c in range(len(steps))]
    block = 16
    me_ref = me.astype(jnp.int32).reshape(1)
    sent, received = [], []

    def send_chunk(c, after):
        step, chunk = steps[c], ns * steps[c]
        piece = pl.pallas_call(
            prep_kernel,
            grid_spec=pltpu.PrefetchScalarGridSpec(
                num_scalar_prefetch=1,
                grid=(chunk // block,),
                in_specs=[
                    pl.BlockSpec(
                        (ser_local, block, depth),
                        lambda i, m, c=c: (0, (m[0] * half + starts[c]) // block + i, 0),
                    ),
                    whole(depth),
                    *[unread] * len(after),
                ],
                out_specs=pl.BlockSpec((block, ser_local, depth), lambda i, m: (i, 0, 0)),
            ),
            out_shape=jax.ShapeDtypeStruct((chunk, ser_local, depth), jnp.bfloat16),
            compiler_params=params(),
            name="prep_path",
        )(me_ref, series_in, norm_gain, *after)
        sent.append(piece)
        received.append(
            lax.all_to_all(
                piece.reshape(ns, step, ser_local, depth),
                "series", split_axis=0, concat_axis=0, tiled=True,
            )
        )

    send_chunk(0, ())

    turned = lambda weight: jnp.transpose(weight, (1, 2, 0))
    group_own = turned(w_group)
    group_a, group_b = from_partner(group_own)
    gate_a, gate_b = from_partner(w_gate)
    out_a, out_b = from_partner(w_out)

    time_own, time_other = [], []

    def time_call(at, count, after):
        call = pl.pallas_call(
            partial(time_kernel, head_size=head_size),
            grid=(count,),
            in_specs=[
                pl.BlockSpec((1, patches, depth), lambda i: (at + i, 0, 0)),
                whole(depth),
                whole(heads_local, 3 * head_size, depth),
                *[unread] * len(after),
            ],
            out_specs=[pl.BlockSpec((1, half, width), lambda i: (i, 0, 0))] * 2,
            out_shape=[jax.ShapeDtypeStruct((count, half, width), jnp.bfloat16)] * 2,
            scratch_shapes=[pltpu.VMEM((1, 3 * width, depth), jnp.bfloat16)],
            compiler_params=params(),
            name="time_path",
            cost_estimate=pl.CostEstimate(
                flops=2 * count * patches * (depth * 3 * width + 4 * patches * width),
                bytes_accessed=count * patches * (depth + width) * 2,
                transcendentals=count * heads_local * patches * patches,
            ),
        )
        own, give = call(series_in, norm_gain, turned(w_time), *after)
        time_other.append(lax.ppermute(give, "mp", swap))
        time_own.append(own)

    send_chunk(1, (sent[0],))
    time_call(0, ser_local, (sent[1],))
    counts = [ser_local]
    out = jnp.zeros((ser_local, patches, width), jnp.bfloat16)
    last = time_own[-1]
    backs = []
    for c, step in enumerate(steps):
        call = pl.pallas_call(
            partial(group_kernel, head_size=head_size),
            grid=(step,),
            in_specs=[
                pl.BlockSpec((ns, 1, ser_local, depth), lambda i: (0, i, 0, 0)),
                whole(*group_own.shape),
                whole(*group_a.shape),
                whole(*group_b.shape),
                whole(*w_gate.shape),
                whole(*gate_a.shape),
                whole(*gate_b.shape),
                whole(n_series, 1),
                whole(1, n_series),
                unread,
            ],
            out_specs=pl.BlockSpec((ns, 1, ser_local, total), lambda i: (0, i, 0, 0)),
            out_shape=jax.ShapeDtypeStruct((ns, step, ser_local, total), jnp.bfloat16),
            scratch_shapes=[
                pltpu.VMEM((nm, 3 * width, depth), jnp.bfloat16),
                pltpu.VMEM((nm, depth, width), jnp.bfloat16),
            ],
            compiler_params=params(),
            name="group_path",
            cost_estimate=pl.CostEstimate(
                flops=2 * step * n_series * (depth * 4 * total + 4 * n_series * total),
                bytes_accessed=step * n_series * (depth + total) * 2,
                transcendentals=step * nm * heads_local * n_series * n_series,
            ),
        )
        group_out = call(
        received[c], group_own, group_a, group_b, w_gate, gate_a, gate_b,
        group_of.reshape(n_series, 1), group_of.reshape(1, n_series), last,
        )
        last = group_out
        backs.append(lax.all_to_all(group_out, "series", split_axis=0, concat_axis=0, tiled=True))

    for c, step in enumerate(steps):
        chunk = ns * step
        back = backs[c].reshape(chunk, ser_local, total)
        at_chunk = lambda i, c=c: (0, starts[c] // block + i, 0)
        call = pl.pallas_call(
            join_kernel,
            grid=(chunk // block,),
            in_specs=[
                pl.BlockSpec((block, ser_local, total), lambda i: (i, 0, 0)),
                *[pl.BlockSpec((n, block, width), at_chunk) for n in counts * 2],
                whole(*w_out.shape),
                whole(*out_a.shape),
                whole(*out_b.shape),
            ],
            out_specs=[pl.BlockSpec((ser_local, block, width), lambda i: (0, i, 0))] * 2,
            out_shape=[jax.ShapeDtypeStruct((ser_local, chunk, width), jnp.bfloat16)] * 2,
            scratch_shapes=[pltpu.VMEM((total, total), jnp.bfloat16)],
            compiler_params=params(),
            name="join_path",
            cost_estimate=pl.CostEstimate(
                flops=2 * chunk * ser_local * total * total,
                bytes_accessed=4 * chunk * ser_local * total * 2,
                transcendentals=0,
            ),
        )
        keep, give = call(back, *time_own, *time_other, w_out, out_a, out_b)
        taken = lax.ppermute(give, "mp", swap)
        out = lax.dynamic_update_slice_in_dim(out, keep, me * half + starts[c], 1)
        out = lax.dynamic_update_slice_in_dim(out, taken, (nm - 1 - me) * half + starts[c], 1)
    return out


def time_attend(time_qkv):
    head_size = time_qkv.shape[-1]
    queries = time_qkv[:, :, :, 0]
    keys_in = time_qkv[:, :, :, 1]
    values_in = time_qkv[:, :, :, 2]
    scores = jnp.einsum(
        "bphd,bqhd->bhpq", queries, keys_in, preferred_element_type=jnp.float32
    ) * head_size ** (-0.5)
    weights = jax.nn.softmax(scores, axis=-1).astype(jnp.bfloat16)
    return jnp.einsum(
        "bhpq,bqhd->bphd", weights, values_in, preferred_element_type=jnp.float32
    ).astype(jnp.bfloat16)


def group_patch(patch_qkv, same_group):
    head_size = patch_qkv.shape[-1]
    queries = patch_qkv[:, :, 0]
    keys_in = patch_qkv[:, :, 1]
    values_in = patch_qkv[:, :, 2]
    scores = jnp.einsum(
        "ihd,jhd->hij", queries, keys_in, preferred_element_type=jnp.float32
    ) * head_size ** (-0.5)
    scores = jnp.where(same_group[None], scores, -1e30)
    weights = jax.nn.softmax(scores, axis=-1).astype(jnp.bfloat16)
    return jnp.einsum(
        "hij,jhd->ihd", weights, values_in, preferred_element_type=jnp.float32
    ).astype(jnp.bfloat16)


def split_heads(series_in, norm_gain, w_time, w_group, w_gate, w_out, group_of):
    ser_local, patches, width = series_in.shape
    heads_local = w_time.shape[1]
    head_size = w_time.shape[2] // 3
    normed = rms_norm(series_in, norm_gain)
    flat_rows = normed.reshape(ser_local * patches, width)
    time_qkv = jnp.dot(
        flat_rows, w_time.reshape(width, -1), preferred_element_type=jnp.float32
    ).astype(jnp.bfloat16)
    time_qkv = time_qkv.reshape(ser_local, patches, heads_local, 3, head_size)
    time_out = time_attend(time_qkv).reshape(ser_local * patches, heads_local * head_size)
    quarter = width // lax.axis_size("mp")
    own_columns = lax.dynamic_slice_in_dim(normed, lax.axis_index("mp") * quarter, quarter, 2)
    moved = lax.all_to_all(own_columns, "series", split_axis=1, concat_axis=0, tiled=True)
    full_rows = lax.all_gather(moved, "mp", axis=2, tiled=True)
    owned = jnp.dot(
        full_rows.reshape(-1, width), w_group.reshape(width, -1), preferred_element_type=jnp.float32
    ).astype(jnp.bfloat16)
    owned = owned.reshape(full_rows.shape[0], full_rows.shape[1], -1)
    all_series, patch_local = (owned.shape[0], owned.shape[1])
    owned = owned.reshape(all_series, patch_local, heads_local, 3, head_size)
    same_group = group_of[:, None] == group_of[None, :]
    group_out = lax.map(partial(group_patch, same_group=same_group), jnp.moveaxis(owned, 1, 0))
    group_out = jnp.moveaxis(group_out, 0, 1).reshape(
        all_series, patch_local, heads_local * head_size
    )
    returned = lax.all_to_all(group_out, "series", split_axis=0, concat_axis=1, tiled=True)
    returned = returned.reshape(ser_local * patches, heads_local * head_size)
    gate_value = jax.nn.sigmoid(jnp.dot(flat_rows, w_gate, preferred_element_type=jnp.float32))
    merged = (time_out.astype(jnp.float32) + gate_value * returned.astype(jnp.float32)).astype(
        jnp.bfloat16
    )
    head_term = jnp.dot(merged, w_out, preferred_element_type=jnp.float32).reshape(
        ser_local, patches, width
    )
    return lax.psum_scatter(head_term.astype(jnp.bfloat16), "mp", scatter_dimension=2, tiled=True)


def per_device(series_in, norm_gain, w_time, *rest):
    ser_local, patches, _ = series_in.shape
    ns, nm = lax.axis_size("series"), lax.axis_size("mp")
    pairs = w_time.shape[1] % 2 == 0 and w_time.shape[2] % 48 == 0 and (2 * w_time.shape[2] // 3) % 128 == 0
    tiled = ser_local % 16 == 0 and patches % (ns * nm * sum(SHARES)) == 0
    tiled = tiled and ns % 16 == 0 and w_time.shape[0] % 32 == 0
    if nm == 2 and pairs and tiled:
        return split_patches(series_in, norm_gain, w_time, *rest)
    return split_heads(series_in, norm_gain, w_time, *rest)


def solution(mesh):
    placed = (
        P("series", None, None),
        P(),
        P(None, "mp", None),
        P(None, "mp", None),
        P(None, "mp"),
        P("mp", None),
        P(),
    )
    return jax.shard_map(
        per_device, mesh=mesh, in_specs=placed, out_specs=P("series", None, "mp"), check_vma=False
    )
```
